256 devices in a mesh: outer: 8 (over z_hi, y), shard: 32 (over z_lo, x, core).
Axes of the slice: x: 4, y: 4, z: 8 (z_hi: 2, z_lo: 4; z = z_hi * 4 + z_lo), core: 2. Of those that a mesh axis runs over, the one named last changes fastest.
Arguments:
- grad_values: bfloat16 [8, 32, 256, 14848], P('outer', 'shard'), may hold values from -6 to 6
- grad_scales: bfloat16 [8, 32, 256, 116], P('outer', 'shard'), may hold values from 0.029907227 to 0.29882812
- block_owner: int32 [256], replicated, may hold values from 0 to 31, as said below
- projector: bfloat16 [8192, 256], P(('outer', 'shard')), may hold values from -0.375 to 0.375
- weights: bfloat16 [8192, 14848], P(('outer', 'shard')), may hold values from -6 to 6
- first_moment: float32 [256, 14848], P('shard'), may hold values from -6 to 6
- second_moment: float32 [256, 14848], P('shard'), may hold values from 0.5 to 4
Outputs:
- new_weights: bfloat16 [8192, 14848], P(('outer', 'shard'))
- new_first: float32 [256, 14848], P('shard')
- new_second: float32 [256, 14848], P('shard')
The draws below stay inside these ranges and needn't reach their ends.
Inputs may be any that keep to these rules, and one draw needn't show every extreme that they name: `block_owner`: every index of shard owns exactly 8 rows.
All inputs are finite; a program needn't handle non-finite values.
Results may differ from the reference program's by a relative error of at most 0.0015.
Values may be sent and summed in bfloat16 or wider, within the bound.
A program may use at most 128 MiB of HBM per device.

```python
import math
import jax
import jax.numpy as jnp
from jax import lax

D = 8192
FFW = 14848
RANK = 256
BLOCK = 128
COL_BLOCKS = 116
ROWS_OWN = 8
N_OUTER = 8
N_SHARD = 32


def draw_block_owner(key, part):
    shuffled = jax.random.permutation(key, RANK)
    return (shuffled // ROWS_OWN).astype(jnp.int32)


def block_levels(key, dims, cuts, least, top_value):
    loudness, own = 1.0, jax.random.fold_in(key, 6)
    for position, parts in cuts:
        heights = jnp.exp(jax.random.uniform(jax.random.fold_in(own, position), (parts,), jnp.float32, least / len(cuts), top_value / len(cuts)))
        loudness = loudness * jnp.repeat(heights, dims[position] // parts).reshape([-1 if axis == position else 1 for axis in range(len(dims))])
    return loudness


def normal_values(rng, extent, scale, limit, shards=(), kind=jnp.bfloat16):
    array = jax.random.normal(rng, extent, jnp.float32) * scale
    if len(shards) > 0:
        array = block_levels(rng, extent, shards, -0.22, 0.18) * array
    return jnp.clip(array, min=-limit, max=limit).astype(kind)


def setup_inputs(seed: int = 0) -> dict:
    splits = jax.random.split(jax.random.key(seed), 8)
    return {
        "grad_values": normal_values(splits[0], (N_OUTER, N_SHARD, RANK, FFW), 1.0, 6.0, ((0, 8), (1, 32))),
        "grad_scales": jnp.clip(jnp.exp(math.log(0.29882812) - 2.30176843 * jax.random.uniform(splits[1], (N_OUTER, N_SHARD, RANK, COL_BLOCKS), jnp.float32) ** block_levels(splits[1], (N_OUTER, N_SHARD, RANK, COL_BLOCKS), ((0, 8), (1, 32)), -0.2, 0.2)), 0.029907227, 0.29882812).astype(jnp.bfloat16),
        "block_owner": draw_block_owner(jax.random.fold_in(splits[7], 71), 0),
        "projector": normal_values(splits[3], (D, RANK), RANK ** -0.5, 0.375, ((0, 256),)),
        "weights": normal_values(splits[4], (D, FFW), 1.0, 6.0, ((0, 256),)),
        "first_moment": normal_values(splits[5], (RANK, FFW), 1.0, 6.0, ((0, 32),), jnp.float32),
        "second_moment": jnp.clip(jnp.exp(math.log(4.0) - 2.0794415 * jax.random.uniform(splits[6], (RANK, FFW), jnp.float32) ** block_levels(splits[6], (RANK, FFW), ((0, 32),), -0.2, 0.2)), 0.5, 4.0),
    }


first_decay = 0.9
second_decay = 0.999
step_count = 100.0
update_scale = 0.25

def reference(grad_values, grad_scales, block_owner, projector, weights, first_moment, second_moment):
    row_order = jnp.argsort(block_owner * RANK + jnp.arange(RANK, dtype=jnp.int32)).astype(jnp.int32)
    inverse = jnp.argsort(row_order).astype(jnp.int32)

    def per_pod(pieces):
        values, scales = pieces
        blocked = values.astype(jnp.float32).reshape(N_SHARD, RANK, COL_BLOCKS, BLOCK)
        pod_sum = lax.optimization_barrier(jnp.sum(blocked * scales.astype(jnp.float32)[..., None], axis=0))
        pod_low = lax.optimization_barrier(pod_sum.astype(jnp.bfloat16))
        return pod_low.astype(jnp.float32)
    grad_low = lax.optimization_barrier(jnp.sum(lax.map(per_pod, (grad_values, grad_scales)), axis=0)).reshape(RANK, FFW)
    owned = grad_low[row_order]
    new_first = first_decay * first_moment + (1.0 - first_decay) * owned
    new_second = second_decay * second_moment + (1.0 - second_decay) * owned * owned
    corrected = new_first / (1.0 - first_decay ** step_count)
    spread = jnp.sqrt(new_second / (1.0 - second_decay ** step_count)) + 1e-08
    update = (corrected / spread).astype(jnp.bfloat16)
    direction = update[inverse]
    change = jnp.dot(projector, direction, preferred_element_type=jnp.float32)
    new_weights = (weights.astype(jnp.float32) - update_scale * change).astype(jnp.bfloat16)
    return (new_weights, new_first, new_second)
```

```python
import functools
import jax
import jax.numpy as jnp
from jax import lax
from jax.experimental import pallas as pl
from jax.experimental.pallas import tpu as pltpu
from jax.sharding import PartitionSpec as P

first_decay = 0.9
second_decay = 0.999
step_count = 100.0
update_scale = 0.25

f32, bf16 = jnp.float32, jnp.bfloat16
MESH = pl.DeviceIdType.MESH

RANK = 256
TILES = 116
HALF = TILES // 2
HC = HALF * 128

PIECES = (
    ("A", 0, 2, -1),
    ("A", 2, 4, -1),
    ("B", 6, 8, -1),
    ("A", 14, 2, -1),
    ("B", 16, 8, 1),
    ("A", 24, 4, 1),
    ("A", 28, 6, -1),
    ("B", 34, 8, 1),
    ("B", 42, 8, -1),
    ("A", 50, 8, 1),
)
ORDER = (
    "0c", "1c", "2c", "0mid", "3c", "4c", "0end", "1mid",
    "5c", "3mid", "6c", "2mid", "7c", "1end", "4mid", "3end",
    "0zsum", "5mid", "8c", "2end", "6mid", "9c", "5end", "1zsum",
    "7mid", "3zsum", "2xsum", "4end", "0ysum", "6end", "8mid", "9mid",
    "5zsum", "1ysum", "2zsum", "0agz", "4xsum", "7end", "8end", "3ysum",
    "5ysum", "0fwd", "9end", "6zsum", "1agz", "2agz", "7xsum", "4zsum",
    "6ysum", "3agz", "0fin", "8xsum", "5agz", "1fwd", "2agx", "3fwd",
    "9zsum", "5fwd", "7zsum", "4agz", "1fin", "3fin", "5fin", "6agz",
    "2fwd", "8zsum", "9ysum", "7agz", "4agx", "6fwd", "2fin", "8agz",
    "7agx", "4fwd", "6fin", "9agz", "8agx", "7fwd", "9fwd", "4fin",
    "8fwd", "9fin", "8fin", "7fin",
)


def messages():
    names = ["sc", "pj", "wb", "m1", "m2"]
    for i, (kind, _, _, _) in enumerate(PIECES):
        names += [f"{i}raw", f"{i}out", f"{i}r1", f"{i}r2", f"{i}r3", f"{i}g1", f"{i}g2", f"{i}g3"]
        names += [f"{i}z{k}" for k in range(1, 8)] + [f"{i}gz{k}" for k in range(1, 8)]
        if kind == "A":
            names += [f"{i}y{k}" for k in range(1, 4)]
            names += [f"{i}o0{z}{c}" for z in range(2) for c in range(2) if z + c]
        else:
            names += [f"{i}x{k}" for k in range(1, 4)] + [f"{i}gx{k}" for k in range(1, 4)]
            names += [
                f"{i}o{y}{z}{c}" for y in range(4) for z in range(2) for c in range(2) if y + z + c
            ]
    return {name: k for k, name in enumerate(names)}


MSG = messages()
LOCAL = {
    name: k
    for k, name in enumerate(
        ["sc", "pj", "wb", "m1", "m2"]
        + [f"{i}{n}" for i in range(len(PIECES)) for n in ("raw", "out", "own")]
    )
}


def scratch():
    v = pltpu.VMEM
    shapes = dict(
        V0=v((RANK, HC), bf16),
        V1=v((RANK, HC), bf16),
        SC0=v((RANK, TILES), bf16),
        SC1=v((RANK, TILES), bf16),
        PJ=v((2, 32, RANK), bf16),
        PL=v((RANK, RANK), bf16),
        PT=v((RANK, RANK), bf16),
        SR0=v((TILES, RANK), bf16),
        SR1=v((TILES, RANK), bf16),
        RE=v((64, RANK), bf16),
        WB=v((2, 32, HC), bf16),
        NW=v((2, 32, HC), bf16),
        M1=v((2, 8, HC), f32),
        M2=v((2, 8, HC), f32),
        S=v((HALF, 4, 4, 16, 128), bf16),
        G=v((HALF, 4, 4, 16, 128), bf16),
        ssem=pltpu.SemaphoreType.DMA((len(MSG),)),
        rsem=pltpu.SemaphoreType.DMA((len(MSG),)),
        lsem=pltpu.SemaphoreType.DMA((len(LOCAL),)),
        near=pltpu.SemaphoreType.REGULAR((3,)),
    )
    for i, (kind, _, w, _) in enumerate(PIECES):
        if kind == "A":
            part, n = (w, 4, 16, 128), w // 2
            shapes[f"X{i}"] = v((w, 4, 16, 128), bf16)
            shapes[f"RY{i}"] = v((4, n, 16, 128), bf16)
        else:
            q = w // 4
            part, n = (q, 4, 4, 16, 128), q // 2
            shapes[f"Y{i}"] = v(part, bf16)
            shapes[f"RX{i}"] = v((4, q, 4, 16, 128), bf16)
            shapes[f"X{i}"] = v((q, 4, 16, 128), bf16)
        for r in ("R1", "R2", "R3", "T"):
            shapes[f"{r}{i}"] = v(part, bf16)
        shapes[f"RZ{i}"] = v((8, n, 16, 128), bf16)
        shapes[f"OW{i}"] = v((2, 8, n * 128), f32)
    return shapes


def kernel(names, owner, vals, scales, proj, weights, m1, m2, out_w, out_o, *refs):
    r = dict(zip(names, refs))
    S, G = r["S"], r["G"]
    o = lax.axis_index("outer")
    s = lax.axis_index("shard")
    c = lax.rem(s, 2)
    x = lax.rem(lax.div(s, 2), 4)
    zl = lax.div(s, 8)
    y = lax.rem(o, 4)
    zh = lax.div(o, 4)
    z = zh * 4 + zl

    def xi(d):
        return lax.rem(x + d + 4, 4)

    def yi(d):
        return lax.rem(y + d + 4, 4)

    def zi(d):
        return lax.rem(z + d + 8, 8)

    def dev(dx=0, dy=0, dz=0, dc=0):
        zz = zi(dz)
        cc = lax.rem(c + dc, 2)
        return (lax.div(zz, 4) * 4 + yi(dy), lax.rem(zz, 4) * 8 + xi(dx) * 2 + cc)

    def col(core, tile):
        return pl.multiple_of(core * HC + tile * 128, 128)

    started = []

    def make(name, src, dst, to):
        k = MSG[name]
        return pltpu.make_async_remote_copy(
            src_ref=src,
            dst_ref=dst,
            send_sem=r["ssem"].at[k],
            recv_sem=r["rsem"].at[k],
            device_id=to,
            device_id_type=MESH,
        )

    def send(name, src, dst, **to):
        copy = make(name, src, dst, dev(**to))
        copy.start()
        started.append(copy)

    def got(name, dst):
        make(name, dst, dst, dev(dc=1)).wait_recv()

    local_copies = {}

    def local(name, src, dst):
        copy = pltpu.make_async_copy(src, dst, r["lsem"].at[LOCAL[name]])
        copy.start()
        local_copies[name] = copy

    def local_wait(name):
        local_copies.pop(name).wait()

    barrier = pltpu.get_barrier_semaphore()
    six = [dict(dx=1), dict(dx=-1), dict(dy=1), dict(dy=-1), dict(dz=1), dict(dz=-1)]
    for to in six + [dict(dc=1)]:
        pl.semaphore_signal(barrier, inc=1, device_id=dev(**to), device_id_type=MESH)

    local("sc", scales, r["SR0"])
    for i, (_, off, w, _) in enumerate(PIECES):
        local(
            f"{i}raw",
            vals.at[:, pl.ds(col(c, off), w * 128)],
            r["V0"].at[:, pl.ds(off * 128, w * 128)],
        )
    local("pj", proj, r["PJ"].at[c])
    local("wb", weights.at[:, pl.ds(col(c, 0), HC)], r["WB"].at[c])
    local("m1", m1.at[:, pl.ds(col(c, 0), HC)], r["M1"].at[c])
    local("m2", m2.at[:, pl.ds(col(c, 0), HC)], r["M2"].at[c])

    pl.semaphore_wait(barrier, 7)
    pc = 1 - c
    send("sc", scales, r["SR1"], dc=1)
    for i, (_, off, w, _) in enumerate(PIECES):
        send(
            f"{i}raw",
            vals.at[:, pl.ds(col(pc, off), w * 128)],
            r["V1"].at[:, pl.ds(off * 128, w * 128)],
            dc=1,
        )
    send("pj", proj, r["PJ"].at[c], dc=1)
    send("m1", m1.at[:, pl.ds(col(pc, 0), HC)], r["M1"].at[c], dc=1)
    send("m2", m2.at[:, pl.ds(col(pc, 0), HC)], r["M2"].at[c], dc=1)
    send("wb", weights.at[:, pl.ds(col(pc, 0), HC)], r["WB"].at[c], dc=1)

    def near_signal(k):
        for to in six if k == 0 else six[4:]:
            pl.semaphore_signal(
                r["near"].at[k], inc=1, device_id=dev(**to), device_id_type=MESH
            )

    def near_wait(k):
        pl.semaphore_wait(r["near"].at[k], 6 if k == 0 else 2)

    near_signal(0)

    rows = lax.broadcasted_iota(jnp.int32, (1, RANK), 1)
    keys = jnp.broadcast_to((owner[...] * RANK + rows).astype(f32), (RANK, RANK))
    keys_t = keys.T
    place = jnp.sum(jnp.where(keys_t < keys, 1.0, 0.0), axis=0, keepdims=True)
    lines = lax.broadcasted_iota(jnp.int32, (RANK, RANK), 0).astype(f32)
    r["PL"][...] = jnp.where(place == lines, 1.0, 0.0).astype(bf16)
    place_t = jnp.sum(jnp.where(keys < keys_t, 1.0, 0.0), axis=1, keepdims=True)
    lanes = lax.broadcasted_iota(jnp.int32, (RANK, RANK), 1).astype(f32)
    r["PT"][...] = jnp.where(place_t == lanes, 1.0, 0.0).astype(bf16)

    def total(terms):
        out = terms[0].astype(f32)
        for term in terms[1:]:
            out = out + term.astype(f32)
        return out

    def compute(i):
        _, off, w, _ = PIECES[i]
        local_wait(f"{i}raw")
        got(f"{i}raw", r["V1"].at[:, pl.ds(off * 128, w * 128)])

        def body(j, carry):
            cols = pl.ds(pl.multiple_of((off + 2 * j) * 128, 256), 256)
            block = lax.broadcasted_iota(jnp.int32, (TILES, 256), 0)
            lane = lax.broadcasted_iota(jnp.int32, (TILES, 256), 1)
            want = c * HALF + off + 2 * j + jnp.where(lane >= 128, 1, 0)
            spread = jnp.where(block == want, 1.0, 0.0).astype(bf16)
            e0 = jnp.dot(r["SC0"][...], spread, preferred_element_type=f32)
            e1 = jnp.dot(r["SC1"][...], spread, preferred_element_type=f32)
            both = r["V0"][:, cols].astype(f32) * e0 + r["V1"][:, cols].astype(f32) * e1
            put = jnp.dot(r["PL"][...], both.astype(bf16), preferred_element_type=f32)
            put = put.astype(bf16)
            S[off + 2 * j] = put[:, :128].reshape(4, 4, 16, 128)
            S[off + 2 * j + 1] = put[:, 128:].reshape(4, 4, 16, 128)
            return carry

        lax.fori_loop(0, w // 2, body, 0)

    def ring(i):
        kind, off, w, sg = PIECES[i]
        if kind == "A":
            return sg, xi, (lambda d: dict(dx=d)), (lambda b, p: b.at[pl.ds(off, w), :, p])
        q = w // 4
        return sg, yi, (lambda d: dict(dy=d)), (lambda b, p: b.at[pl.ds(off + p * q, q)])

    def piece_loop(n, body):
        def step(t, carry):
            body(t)
            return carry

        lax.fori_loop(0, n, step, 0)

    def start(i):
        sg, at, to, part = ring(i)
        send(f"{i}r1", part(S, at(2 * sg)), r[f"R1{i}"], **to(sg))
        send(f"{i}r3", part(S, at(-sg)), r[f"R3{i}"], **to(-sg))

    def own_part(i):
        kind, off, w, _ = PIECES[i]
        if kind == "A":
            return w, lambda p, t: S[off + t, :, p]
        q = w // 4
        return q, lambda p, t: S[off + p * q + t]

    def mid(i):
        sg, at, to, part = ring(i)
        got(f"{i}r1", r[f"R1{i}"])
        n, own = own_part(i)
        p = at(sg)

        def body(t):
            r[f"T{i}"][t] = total([own(p, t), r[f"R1{i}"][t]]).astype(bf16)

        piece_loop(n, body)
        send(f"{i}r2", r[f"T{i}"], r[f"R2{i}"], **to(sg))

    def end(i):
        kind = PIECES[i][0]
        got(f"{i}r3", r[f"R3{i}"])
        got(f"{i}r2", r[f"R2{i}"])
        n, own = own_part(i)
        p = x if kind == "A" else y
        dst = r[f"X{i}"] if kind == "A" else r[f"Y{i}"]

        def body(t):
            dst[t] = total([own(p, t), r[f"R3{i}"][t], r[f"R2{i}"][t]]).astype(bf16)

        piece_loop(n, body)
        if kind == "A":
            z_send(i)
        else:
            for k in range(1, 4):
                send(f"{i}x{k}", dst.at[:, :, xi(k)], r[f"RX{i}"].at[x], dx=k)

    def xsum(i):
        for k in range(1, 4):
            got(f"{i}x{k}", r[f"RX{i}"].at[xi(-k)])

        def body(t):
            terms = [r[f"Y{i}"][t, :, x]] + [r[f"RX{i}"][xi(-k), t] for k in range(1, 4)]
            r[f"X{i}"][t] = total(terms).astype(bf16)

        piece_loop(PIECES[i][2] // 4, body)
        z_send(i)

    def z_tiles(i):
        kind, _, w, _ = PIECES[i]
        return w // 2 if kind == "A" else w // 8

    def z_send(i):
        n = z_tiles(i)
        for k in range(1, 8):
            zz = zi(k)
            src = r[f"X{i}"].at[pl.ds(lax.div(zz, 4) * n, n), lax.rem(zz, 4)]
            send(f"{i}z{k}", src, r[f"RZ{i}"].at[z], dz=k)

    def z_terms(i, t):
        n = z_tiles(i)
        terms = [r[f"X{i}"][zh * n + t, zl]]
        return terms + [r[f"RZ{i}"][zi(-k), t] for k in range(1, 8)]

    def z_got(i):
        for k in range(1, 8):
            got(f"{i}z{k}", r[f"RZ{i}"].at[zi(-k)])

    def first_tile(i, yy, hh):
        kind, off, w, _ = PIECES[i]
        if kind == "A":
            return off + hh * (w // 2)
        return off + yy * (w // 4) + hh * (w // 8)

    def update(i, owned_of):
        n = z_tiles(i)
        tile0 = first_tile(i, y, zh)

        def body(t):
            owned = owned_of(t)
            cols = pl.ds(pl.multiple_of((tile0 + t) * 128, 128), 128)
            dirs = []
            for h in range(2):
                part = owned[8 * h : 8 * h + 8]
                r[f"OW{i}"][h, :, pl.ds(pl.multiple_of(t * 128, 128), 128)] = part
                nf = first_decay * r["M1"][h, :, cols] + (1.0 - first_decay) * part
                ns = second_decay * r["M2"][h, :, cols] + (1.0 - second_decay) * part * part
                corrected = nf / (1.0 - first_decay**step_count)
                spread = jnp.sqrt(ns / (1.0 - second_decay**step_count)) + 1e-08
                dirs.append(corrected / spread)
            G[tile0 + t, zl, x] = jnp.concatenate(dirs, axis=0).astype(bf16)

        piece_loop(n, body)
        mine = G.at[pl.ds(tile0, n), zl, x]
        for k in range(1, 8):
            send(f"{i}gz{k}", mine, mine, dz=k)
        cols = pl.ds(col(c, tile0), n * 128)
        local(f"{i}own", r[f"OW{i}"].at[c], out_o.at[:, cols])
        for dy in range(4 if PIECES[i][0] == "B" else 1):
            for dz in range(2):
                for dc in range(2):
                    if dy + dz + dc:
                        src = r[f"OW{i}"].at[pc if dc else c]
                        send(
                            f"{i}o{dy}{dz}{dc}", src, out_o.at[:, cols], dy=dy, dz=4 * dz, dc=dc
                        )

    def owned_got(i):
        n = z_tiles(i)
        for dy in range(4 if PIECES[i][0] == "B" else 1):
            for dz in range(2):
                for dc in range(2):
                    if dy + dz + dc:
                        tile = first_tile(i, yi(-dy), (1 - zh) if dz else zh)
                        cols = pl.ds(col(pc if dc else c, tile), n * 128)
                        got(f"{i}o{dy}{dz}{dc}", out_o.at[:, cols])

    def zsum_a(i):
        z_got(i)

        def body(t):
            r[f"RY{i}"][y, t] = total(z_terms(i, t)).astype(bf16)

        piece_loop(z_tiles(i), body)
        for k in range(1, 4):
            send(f"{i}y{k}", r[f"RY{i}"].at[y], r[f"RY{i}"].at[y], dy=k)

    def ysum(i):
        for k in range(1, 4):
            got(f"{i}y{k}", r[f"RY{i}"].at[yi(-k)])
        update(i, lambda t: total([r[f"RY{i}"][k, t] for k in range(4)]))

    def zsum_b(i):
        z_got(i)
        update(i, lambda t: total(z_terms(i, t)))

    def gather_z_got(i):
        n = z_tiles(i)
        for k in range(1, 8):
            zz = zi(-k)
            tile = first_tile(i, y, lax.div(zz, 4))
            got(f"{i}gz{k}", G.at[pl.ds(tile, n), lax.rem(zz, 4), x])

    def last_ring(i):
        sg, at, to, part = ring(i)
        mine = part(G, at(0))
        send(f"{i}g1", mine, mine, **to(sg))
        send(f"{i}g3", mine, mine, **to(-sg))

    def agz(i):
        gather_z_got(i)
        kind, off, w, _ = PIECES[i]
        if kind == "A":
            last_ring(i)
        else:
            q = w // 4
            mine = G.at[pl.ds(off + y * q, q), :, x]
            for k in range(1, 4):
                send(f"{i}gx{k}", mine, mine, dx=k)

    def agx(i):
        _, off, w, _ = PIECES[i]
        q = w // 4
        for k in range(1, 4):
            got(f"{i}gx{k}", G.at[pl.ds(off + y * q, q), :, xi(-k)])
        last_ring(i)

    def fwd(i):
        sg, at, to, part = ring(i)
        behind = part(G, at(-sg))
        got(f"{i}g1", behind)
        send(f"{i}g2", behind, behind, **to(sg))

    def fin(i):
        _, off, w, _ = PIECES[i]
        sg, at, to, part = ring(i)
        got(f"{i}g3", part(G, at(sg)))
        got(f"{i}g2", part(G, at(2 * sg)))

        def body(j, carry):
            cols = pl.ds(pl.multiple_of((off + 2 * j) * 128, 256), 256)
            u = jnp.concatenate(
                [G[off + 2 * j].reshape(256, 128), G[off + 2 * j + 1].reshape(256, 128)], axis=1
            )
            change = jnp.dot(r["RE"][...], u, preferred_element_type=f32)
            old = r["WB"][:, :, cols].reshape(64, 256).astype(f32)
            new = (old - update_scale * change).astype(bf16)
            r["NW"][:, :, cols] = new.reshape(2, 32, 256)
            return carry

        lax.fori_loop(0, w // 2, body, 0)
        here = pl.ds(off * 128, w * 128)
        there = pl.ds(col(c, off), w * 128)
        send(f"{i}out", r["NW"].at[pc, :, here], out_w.at[:, there], dc=1)
        local(f"{i}out", r["NW"].at[c, :, here], out_w.at[:, there])

    actions = dict(
        mid=mid, end=end, xsum=xsum, ysum=ysum, agz=agz, agx=agx, fwd=fwd, fin=fin
    )
    local_wait("sc")
    got("sc", r["SR1"])
    for src, dst in (("SR0", "SC0"), ("SR1", "SC1")):
        r[dst][...] = r[src][...].astype(f32).T.astype(bf16)
    computed = 0
    updating = {"A": "ysum", "B": "zsum"}
    have_moments = have_weights = False
    for item in ORDER:
        i, what = int(item[0]), item[1:]
        if what == updating[PIECES[i][0]] and not have_moments:
            have_moments = True
            for name in ("m1", "m2"):
                local_wait(name)
            got("m1", r["M1"].at[pc])
            got("m2", r["M2"].at[pc])
        if what == "fin" and not have_weights:
            have_weights = True
            for name in ("pj", "wb"):
                local_wait(name)
            got("pj", r["PJ"].at[pc])
            got("wb", r["WB"].at[pc])
            reordered = jnp.dot(
                r["PJ"][...].reshape(64, RANK), r["PT"][...], preferred_element_type=f32
            )
            r["RE"][...] = reordered.astype(bf16)
        if what == "c":
            compute(i)
            start(i)
            if computed < 3:
                near_wait(computed)
                if computed < 2:
                    near_signal(computed + 1)
            computed += 1
        elif what == "zsum":
            (zsum_a if PIECES[i][0] == "A" else zsum_b)(i)
        else:
            actions[what](i)

    for i, (_, off, w, _) in enumerate(PIECES):
        owned_got(i)
        got(f"{i}out", out_w.at[:, pl.ds(col(pc, off), w * 128)])
    for name in list(local_copies):
        local_wait(name)
    for copy in started:
        copy.wait_send()


def per_device(
    grad_values, grad_scales, block_owner, projector, weights, first_moment, second_moment
):
    shapes = scratch()
    any_spec = pl.BlockSpec(memory_space=pl.ANY)
    new_weights, owned = pl.pallas_call(
        functools.partial(kernel, tuple(shapes)),
        out_shape=(
            jax.ShapeDtypeStruct(weights.shape, bf16),
            jax.ShapeDtypeStruct(first_moment.shape, f32),
        ),
        in_specs=[pl.BlockSpec(memory_space=pltpu.VMEM)] + [any_spec] * 6,
        out_specs=(any_spec, any_spec),
        scratch_shapes=list(shapes.values()),
        compiler_params=pltpu.CompilerParams(
            collective_id=0, has_side_effects=True, vmem_limit_bytes=60 * 1024 * 1024
        ),
    )(
        block_owner.reshape(1, RANK),
        grad_values[0, 0],
        grad_scales[0, 0].T,
        projector,
        weights,
        first_moment,
        second_moment,
    )
    new_first = first_decay * first_moment + (1.0 - first_decay) * owned
    new_second = second_decay * second_moment + (1.0 - second_decay) * owned * owned
    return (new_weights, new_first, new_second)


def solution(mesh):
    placed = (
        P("outer", "shard", None, None),
        P("outer", "shard", None, None),
        P(),
        P(("outer", "shard"), None),
        P(("outer", "shard"), None),
        P("shard", None),
        P("shard", None),
    )
    return jax.shard_map(
        per_device,
        mesh=mesh,
        in_specs=placed,
        out_specs=(P(("outer", "shard"), None), P("shard", None), P("shard", None)),
        check_vma=False,
    )
```

```python
import functools
import math
import jax
import jax.numpy as jnp
from jax import lax
from jax.experimental import pallas as pl
from jax.experimental.pallas import tpu as pltpu
from jax.sharding import PartitionSpec as P

first_decay = 0.9
second_decay = 0.999
step_count = 100.0
update_scale = 0.25

f32, bf16 = jnp.float32, jnp.bfloat16
MESH = pl.DeviceIdType.MESH

RANK = 256
TILES = 116
HALF = TILES // 2
HC = HALF * 128

PIECES = (
    ("A", 0, 2, -1),
    ("A", 2, 4, -1),
    ("B", 6, 8, -1),
    ("A", 14, 2, -1),
    ("B", 16, 8, 1),
    ("A", 24, 4, 1),
    ("A", 28, 6, -1),
    ("B", 34, 8, 1),
    ("B", 42, 8, -1),
    ("A", 50, 8, 1),
)
ORDER = (
    "0c", "1c", "2c", "0mid", "3c", "4c", "0end", "1mid",
    "5c", "3mid", "6c", "2mid", "7c", "1end", "4mid", "3end",
    "0zsum", "5mid", "8c", "2end", "6mid", "9c", "5end", "1zsum",
    "7mid", "3zsum", "2xsum", "4end", "0ysum", "6end", "8mid", "9mid",
    "5zsum", "1ysum", "2zsum", "0agz", "4xsum", "7end", "8end", "3ysum",
    "5ysum", "0fwd", "9end", "6zsum", "1agz", "2agz", "7xsum", "4zsum",
    "6ysum", "3agz", "0fin", "8xsum", "5agz", "1fwd", "2agx", "3fwd",
    "9zsum", "5fwd", "7zsum", "4agz", "1fin", "3fin", "5fin", "6agz",
    "2fwd", "8zsum", "9ysum", "7agz", "4agx", "6fwd", "2fin", "8agz",
    "7agx", "4fwd", "6fin", "9agz", "8agx", "7fwd", "9fwd", "4fin",
    "8fwd", "9fin", "8fin", "7fin",
)


def keys():
    names = ["sc", "pj", "wb", "m1", "m2", "o", "out"]
    for i, (kind, _, _, _) in enumerate(PIECES):
        names += [f"{i}{n}" for n in ("raw", "r1", "r23", "z", "gz", "g1", "g23")]
        names += [f"{i}y"] if kind == "A" else [f"{i}x", f"{i}gx"]
    return {name: k for k, name in enumerate(names)}


KEYS = keys()


def key_of(name):
    if not name[0].isdigit():
        return KEYS[name]
    i, what = name[0], name[1:]
    if what == "out":
        return KEYS["out"]
    if what[0] == "o":
        return KEYS["o"]
    pairs = dict(raw="raw", r1="r1", r2="r23", r3="r23", g1="g1", g2="g23", g3="g23")
    return KEYS[i + pairs.get(what, what[:-1])]


def send_group(name):
    if not name[0].isdigit():
        return {"sc": "sc", "wb": "wb"}.get(name, "pm")
    i, what = name[0], name[1:]
    if what[0] == "o":
        return "out" if what == "out" else "o"
    return i + ("big" if what in ("raw", "r1", "r2", "r3", "g1", "g2", "g3") else "small")


GROUPS = ["sc", "wb", "pm", "out", "o"]
GROUPS += [f"{i}{n}" for i in range(len(PIECES)) for n in ("big", "small")]
GROUPS = {name: k for k, name in enumerate(GROUPS)}


def extents(tiles):
    for bb in (4, 3, 2, 1):
        for cc in (4, 3, 2, 1):
            if tiles % (bb * cc) == 0 and tiles // (bb * cc) <= HALF:
                return tiles // (bb * cc), bb, cc
    raise ValueError(tiles)


def scratch():
    v = pltpu.VMEM
    shapes = dict(
        V=v((2, RANK, HC), bf16),
        SC0=v((RANK, TILES), bf16),
        SC1=v((RANK, TILES), bf16),
        PJ=v((2, 32, RANK), bf16),
        PL=v((RANK, RANK), bf16),
        PT=v((RANK, RANK), bf16),
        SR=v((2, TILES, RANK), bf16),
        RE=v((64, RANK), bf16),
        WB=v((2, 32, HC), bf16),
        NW=v((2, 32, HC), bf16),
        M1=v((2, 8, HC), f32),
        M2=v((2, 8, HC), f32),
        S=v((HALF, 4, 4, 16, 128), bf16),
        G=v((HALF, 4, 4, 16, 128), bf16),
        ssem=pltpu.SemaphoreType.DMA((len(GROUPS),)),
        rsem=pltpu.SemaphoreType.DMA((len(KEYS),)),
        near=pltpu.SemaphoreType.REGULAR((3,)),
    )
    for i, (kind, _, w, _) in enumerate(PIECES):
        if kind == "A":
            part, n = (w, 4, 16, 128), w // 2
            shapes[f"X{i}"] = v((w, 4, 16, 128), bf16)
            shapes[f"RY{i}"] = v((4, n, 16, 128), bf16)
        else:
            q = w // 4
            part, n = (q, 4, 4, 16, 128), q // 2
            shapes[f"Y{i}"] = v(part, bf16)
            shapes[f"RX{i}"] = v((4, q, 4, 16, 128), bf16)
            shapes[f"X{i}"] = v((q, 4, 16, 128), bf16)
        shapes[f"R1{i}"] = shapes[f"T{i}"] = v(part, bf16)
        shapes[f"R23{i}"] = v((2,) + part, bf16)
        shapes[f"RZ{i}"] = v((8, n, 16, 128), bf16)
        shapes[f"OW{i}"] = v((2, 8, n * 128), f32)
    return shapes


def kernel(names, owner, vals, scales, proj, weights, m1, m2, out_w, out_o, *refs):
    r = dict(zip(names, refs))
    S, G = r["S"], r["G"]
    o = lax.axis_index("outer")
    s = lax.axis_index("shard")
    c = lax.rem(s, 2)
    x = lax.rem(lax.div(s, 2), 4)
    zl = lax.div(s, 8)
    y = lax.rem(o, 4)
    zh = lax.div(o, 4)
    z = zh * 4 + zl

    def xi(d):
        return lax.rem(x + d + 4, 4)

    def yi(d):
        return lax.rem(y + d + 4, 4)

    def zi(d):
        return lax.rem(z + d + 8, 8)

    def dev(dx=0, dy=0, dz=0, dc=0):
        zz = zi(dz)
        cc = lax.rem(c + dc, 2)
        return (lax.div(zz, 4) * 4 + yi(dy), lax.rem(zz, 4) * 8 + xi(dx) * 2 + cc)

    def col(core, tile):
        return pl.multiple_of(core * HC + tile * 128, 128)

    sent = {}

    def make(name, src, dst, to):
        return pltpu.make_async_remote_copy(
            src_ref=src,
            dst_ref=dst,
            send_sem=r["ssem"].at[GROUPS[send_group(name)]],
            recv_sem=r["rsem"].at[key_of(name)],
            device_id=to,
            device_id_type=MESH,
        )

    def send(name, src, dst, **to):
        copy = make(name, src, dst, dev(**to))
        copy.start()
        group = send_group(name)
        size = math.prod(src.shape) * src.dtype.itemsize
        sent[group] = sent.get(group, 0) + size

    def got(name, dst):
        pltpu.make_async_copy(dst, dst, r["rsem"].at[key_of(name)]).wait()

    def local(name, src, dst):
        pltpu.make_async_copy(src, dst, r["rsem"].at[key_of(name)]).start()

    barrier = pltpu.get_barrier_semaphore()
    six = [dict(dx=1), dict(dx=-1), dict(dy=1), dict(dy=-1), dict(dz=1), dict(dz=-1)]
    for to in six + [dict(dc=1)]:
        pl.semaphore_signal(barrier, inc=1, device_id=dev(**to), device_id_type=MESH)

    local("sc", scales, r["SR"].at[0])
    for i, (_, off, w, _) in enumerate(PIECES):
        local(
            f"{i}raw",
            vals.at[:, pl.ds(col(c, off), w * 128)],
            r["V"].at[0, :, pl.ds(off * 128, w * 128)],
        )
    local("pj", proj, r["PJ"].at[c])
    local("wb", weights.at[:, pl.ds(col(c, 0), HC)], r["WB"].at[c])
    local("m1", m1.at[:, pl.ds(col(c, 0), HC)], r["M1"].at[c])
    local("m2", m2.at[:, pl.ds(col(c, 0), HC)], r["M2"].at[c])

    pl.semaphore_wait(barrier, 7)
    pc = 1 - c
    send("sc", scales, r["SR"].at[1], dc=1)
    for i, (_, off, w, _) in enumerate(PIECES):
        send(
            f"{i}raw",
            vals.at[:, pl.ds(col(pc, off), w * 128)],
            r["V"].at[1, :, pl.ds(off * 128, w * 128)],
            dc=1,
        )
    send("pj", proj, r["PJ"].at[c], dc=1)
    send("m1", m1.at[:, pl.ds(col(pc, 0), HC)], r["M1"].at[c], dc=1)
    send("m2", m2.at[:, pl.ds(col(pc, 0), HC)], r["M2"].at[c], dc=1)
    send("wb", weights.at[:, pl.ds(col(pc, 0), HC)], r["WB"].at[c], dc=1)

    def near_signal(k):
        for to in six if k == 0 else six[4:]:
            pl.semaphore_signal(
                r["near"].at[k], inc=1, device_id=dev(**to), device_id_type=MESH
            )

    def near_wait(k):
        pl.semaphore_wait(r["near"].at[k], 6 if k == 0 else 2)

    near_signal(0)

    rows = lax.broadcasted_iota(jnp.int32, (1, RANK), 1)
    keys = jnp.broadcast_to((owner[...] * RANK + rows).astype(f32), (RANK, RANK))
    keys_t = keys.T
    place = jnp.sum(jnp.where(keys_t < keys, 1.0, 0.0), axis=0, keepdims=True)
    lines = lax.broadcasted_iota(jnp.int32, (RANK, RANK), 0).astype(f32)
    r["PL"][...] = jnp.where(place == lines, 1.0, 0.0).astype(bf16)
    place_t = jnp.sum(jnp.where(keys < keys_t, 1.0, 0.0), axis=1, keepdims=True)
    lanes = lax.broadcasted_iota(jnp.int32, (RANK, RANK), 1).astype(f32)
    r["PT"][...] = jnp.where(place_t == lanes, 1.0, 0.0).astype(bf16)

    def total(terms):
        out = terms[0].astype(f32)
        for term in terms[1:]:
            out = out + term.astype(f32)
        return out

    def compute(i):
        _, off, w, _ = PIECES[i]
        got(f"{i}raw", r["V"].at[:, :, pl.ds(off * 128, w * 128)])

        def body(j, carry):
            cols = pl.ds(pl.multiple_of((off + 2 * j) * 128, 256), 256)
            block = lax.broadcasted_iota(jnp.int32, (TILES, 256), 0)
            lane = lax.broadcasted_iota(jnp.int32, (TILES, 256), 1)
            want = c * HALF + off + 2 * j + jnp.where(lane >= 128, 1, 0)
            spread = jnp.where(block == want, 1.0, 0.0).astype(bf16)
            e0 = jnp.dot(r["SC0"][...], spread, preferred_element_type=f32)
            e1 = jnp.dot(r["SC1"][...], spread, preferred_element_type=f32)
            both = r["V"][0, :, cols].astype(f32) * e0 + r["V"][1, :, cols].astype(f32) * e1
            put = jnp.dot(r["PL"][...], both.astype(bf16), preferred_element_type=f32)
            put = put.astype(bf16)
            S[off + 2 * j] = put[:, :128].reshape(4, 4, 16, 128)
            S[off + 2 * j + 1] = put[:, 128:].reshape(4, 4, 16, 128)
            return carry

        lax.fori_loop(0, w // 2, body, 0)

    def ring(i):
        kind, off, w, sg = PIECES[i]
        if kind == "A":
            return sg, xi, (lambda d: dict(dx=d)), (lambda b, p: b.at[pl.ds(off, w), :, p])
        q = w // 4
        return sg, yi, (lambda d: dict(dy=d)), (lambda b, p: b.at[pl.ds(off + p * q, q)])

    def piece_loop(n, body):
        def step(t, carry):
            body(t)
            return carry

        lax.fori_loop(0, n, step, 0)

    def start(i):
        sg, at, to, part = ring(i)
        send(f"{i}r1", part(S, at(2 * sg)), r[f"R1{i}"], **to(sg))
        send(f"{i}r3", part(S, at(-sg)), r[f"R23{i}"].at[1], **to(-sg))

    def own_part(i):
        kind, off, w, _ = PIECES[i]
        if kind == "A":
            return w, lambda p, t: S[off + t, :, p]
        q = w // 4
        return q, lambda p, t: S[off + p * q + t]

    def mid(i):
        sg, at, to, part = ring(i)
        got(f"{i}r1", r[f"R1{i}"])
        n, own = own_part(i)
        p = at(sg)

        def body(t):
            r[f"T{i}"][t] = total([own(p, t), r[f"R1{i}"][t]]).astype(bf16)

        piece_loop(n, body)
        send(f"{i}r2", r[f"T{i}"], r[f"R23{i}"].at[0], **to(sg))

    def end(i):
        kind = PIECES[i][0]
        got(f"{i}r3", r[f"R23{i}"])
        n, own = own_part(i)
        p = x if kind == "A" else y
        dst = r[f"X{i}"] if kind == "A" else r[f"Y{i}"]

        def body(t):
            dst[t] = total([own(p, t), r[f"R23{i}"][0, t], r[f"R23{i}"][1, t]]).astype(bf16)

        piece_loop(n, body)
        if kind == "A":
            z_send(i)
        else:
            for k in range(1, 4):
                send(f"{i}x{k}", dst.at[:, :, xi(k)], r[f"RX{i}"].at[x], dx=k)

    def xsum(i):
        got(f"{i}x1", r[f"RX{i}"].at[pl.ds(0, 3)])

        def body(t):
            terms = [r[f"Y{i}"][t, :, x]] + [r[f"RX{i}"][xi(-k), t] for k in range(1, 4)]
            r[f"X{i}"][t] = total(terms).astype(bf16)

        piece_loop(PIECES[i][2] // 4, body)
        z_send(i)

    def z_tiles(i):
        kind, _, w, _ = PIECES[i]
        return w // 2 if kind == "A" else w // 8

    def z_send(i):
        n = z_tiles(i)
        for k in range(1, 8):
            zz = zi(k)
            src = r[f"X{i}"].at[pl.ds(lax.div(zz, 4) * n, n), lax.rem(zz, 4)]
            send(f"{i}z{k}", src, r[f"RZ{i}"].at[z], dz=k)

    def z_terms(i, t):
        n = z_tiles(i)
        terms = [r[f"X{i}"][zh * n + t, zl]]
        return terms + [r[f"RZ{i}"][zi(-k), t] for k in range(1, 8)]

    def z_got(i):
        got(f"{i}z1", r[f"RZ{i}"].at[pl.ds(0, 7)])

    def first_tile(i, yy, hh):
        kind, off, w, _ = PIECES[i]
        if kind == "A":
            return off + hh * (w // 2)
        return off + yy * (w // 4) + hh * (w // 8)

    def update(i, owned_of):
        n = z_tiles(i)
        tile0 = first_tile(i, y, zh)

        def body(t):
            owned = owned_of(t)
            cols = pl.ds(pl.multiple_of((tile0 + t) * 128, 128), 128)
            dirs = []
            for h in range(2):
                part = owned[8 * h : 8 * h + 8]
                r[f"OW{i}"][h, :, pl.ds(pl.multiple_of(t * 128, 128), 128)] = part
                nf = first_decay * r["M1"][h, :, cols] + (1.0 - first_decay) * part
                ns = second_decay * r["M2"][h, :, cols] + (1.0 - second_decay) * part * part
                corrected = nf / (1.0 - first_decay**step_count)
                spread = jnp.sqrt(ns / (1.0 - second_decay**step_count)) + 1e-08
                dirs.append(corrected / spread)
            G[tile0 + t, zl, x] = jnp.concatenate(dirs, axis=0).astype(bf16)

        piece_loop(n, body)
        mine = G.at[pl.ds(tile0, n), zl, x]
        for k in range(1, 8):
            send(f"{i}gz{k}", mine, mine, dz=k)
        cols = pl.ds(col(c, tile0), n * 128)
        local(f"{i}o000", r[f"OW{i}"].at[c], out_o.at[:, cols])
        for dy in range(4 if PIECES[i][0] == "B" else 1):
            for dz in range(2):
                for dc in range(2):
                    if dy + dz + dc:
                        src = r[f"OW{i}"].at[pc if dc else c]
                        send(
                            f"{i}o{dy}{dz}{dc}", src, out_o.at[:, cols], dy=dy, dz=4 * dz, dc=dc
                        )

    def zsum_a(i):
        z_got(i)

        def body(t):
            r[f"RY{i}"][y, t] = total(z_terms(i, t)).astype(bf16)

        piece_loop(z_tiles(i), body)
        for k in range(1, 4):
            send(f"{i}y{k}", r[f"RY{i}"].at[y], r[f"RY{i}"].at[y], dy=k)

    def ysum(i):
        got(f"{i}y1", r[f"RY{i}"].at[pl.ds(0, 3)])
        update(i, lambda t: total([r[f"RY{i}"][k, t] for k in range(4)]))

    def zsum_b(i):
        z_got(i)
        update(i, lambda t: total(z_terms(i, t)))

    def gather_z_got(i):
        a, bb, cc = extents(7 * z_tiles(i))
        got(f"{i}gz1", S.at[pl.ds(0, a), pl.ds(0, bb), pl.ds(0, cc)])

    def last_ring(i):
        sg, at, to, part = ring(i)
        mine = part(G, at(0))
        send(f"{i}g1", mine, mine, **to(sg))
        send(f"{i}g3", mine, mine, **to(-sg))

    def agz(i):
        gather_z_got(i)
        kind, off, w, _ = PIECES[i]
        if kind == "A":
            last_ring(i)
        else:
            q = w // 4
            mine = G.at[pl.ds(off + y * q, q), :, x]
            for k in range(1, 4):
                send(f"{i}gx{k}", mine, mine, dx=k)

    def agx(i):
        _, off, w, _ = PIECES[i]
        q = w // 4
        got(f"{i}gx1", G.at[pl.ds(off, q), :, pl.ds(0, 3)])
        last_ring(i)

    def fwd(i):
        sg, at, to, part = ring(i)
        behind = part(G, at(-sg))
        got(f"{i}g1", behind)
        send(f"{i}g2", behind, behind, **to(sg))

    def fin(i):
        _, off, w, _ = PIECES[i]
        sg, at, to, part = ring(i)
        if PIECES[i][0] == "A":
            got(f"{i}g3", G.at[pl.ds(off, w), :, pl.ds(0, 2)])
        else:
            got(f"{i}g3", G.at[pl.ds(off, w // 2)])

        def body(j, carry):
            cols = pl.ds(pl.multiple_of((off + 2 * j) * 128, 256), 256)
            u = jnp.concatenate(
                [G[off + 2 * j].reshape(256, 128), G[off + 2 * j + 1].reshape(256, 128)], axis=1
            )
            change = jnp.dot(r["RE"][...], u, preferred_element_type=f32)
            old = r["WB"][:, :, cols].reshape(64, 256).astype(f32)
            new = (old - update_scale * change).astype(bf16)
            r["NW"][:, :, cols] = new.reshape(2, 32, 256)
            return carry

        lax.fori_loop(0, w // 2, body, 0)
        here = pl.ds(off * 128, w * 128)
        there = pl.ds(col(c, off), w * 128)
        send(f"{i}out", r["NW"].at[pc, :, here], out_w.at[:, there], dc=1)
        local(f"{i}out", r["NW"].at[c, :, here], out_w.at[:, there])

    actions = dict(
        mid=mid, end=end, xsum=xsum, ysum=ysum, agz=agz, agx=agx, fwd=fwd, fin=fin
    )
    got("sc", r["SR"])
    for k in range(2):
        r[f"SC{k}"][...] = r["SR"][k].astype(f32).T.astype(bf16)
    computed = 0
    updating = {"A": "ysum", "B": "zsum"}
    have_moments = have_weights = False
    for item in ORDER:
        i, what = int(item[0]), item[1:]
        if what == updating[PIECES[i][0]] and not have_moments:
            have_moments = True
            got("m1", r["M1"])
            got("m2", r["M2"])
        if what == "fin" and not have_weights:
            have_weights = True
            got("pj", r["PJ"])
            got("wb", r["WB"])
            reordered = jnp.dot(
                r["PJ"][...].reshape(64, RANK), r["PT"][...], preferred_element_type=f32
            )
            r["RE"][...] = reordered.astype(bf16)
        if what == "c":
            compute(i)
            start(i)
            if computed < 3:
                near_wait(computed)
                if computed < 2:
                    near_signal(computed + 1)
            computed += 1
        elif what == "zsum":
            (zsum_a if PIECES[i][0] == "A" else zsum_b)(i)
        else:
            actions[what](i)

    got("o", out_o)
    got("out", out_w)
    for group, size in sent.items():
        if group == "sc":
            whole = r["SR"].at[0]
        else:
            a, bb, cc = extents(size // 4096)
            whole = S.at[pl.ds(0, a), pl.ds(0, bb), pl.ds(0, cc)]
        pltpu.make_async_copy(whole, whole, r["ssem"].at[GROUPS[group]]).wait()


def per_device(
    grad_values, grad_scales, block_owner, projector, weights, first_moment, second_moment
):
    shapes = scratch()
    any_spec = pl.BlockSpec(memory_space=pl.ANY)
    new_weights, owned = pl.pallas_call(
        functools.partial(kernel, tuple(shapes)),
        out_shape=(
            jax.ShapeDtypeStruct(weights.shape, bf16),
            jax.ShapeDtypeStruct(first_moment.shape, f32),
        ),
        in_specs=[pl.BlockSpec(memory_space=pltpu.VMEM)] + [any_spec] * 6,
        out_specs=(any_spec, any_spec),
        scratch_shapes=list(shapes.values()),
        compiler_params=pltpu.CompilerParams(
            collective_id=0, has_side_effects=True, vmem_limit_bytes=60 * 1024 * 1024
        ),
    )(
        block_owner.reshape(1, RANK),
        grad_values[0, 0],
        grad_scales[0, 0].T,
        projector,
        weights,
        first_moment,
        second_moment,
    )
    new_first = first_decay * first_moment + (1.0 - first_decay) * owned
    new_second = second_decay * second_moment + (1.0 - second_decay) * owned * owned
    return (new_weights, new_first, new_second)


def solution(mesh):
    placed = (
        P("outer", "shard", None, None),
        P("outer", "shard", None, None),
        P(),
        P(("outer", "shard"), None),
        P(("outer", "shard"), None),
        P("shard", None),
        P("shard", None),
    )
    return jax.shard_map(
        per_device,
        mesh=mesh,
        in_specs=placed,
        out_specs=(P(("outer", "shard"), None), P("shard", None), P("shard", None)),
        check_vma=False,
    )
```

```python
import functools
import math
import jax
import jax.numpy as jnp
from jax import lax
from jax.experimental import pallas as pl
from jax.experimental.pallas import tpu as pltpu
from jax.sharding import PartitionSpec as P

first_decay = 0.9
second_decay = 0.999
step_count = 100.0
update_scale = 0.25

f32, bf16 = jnp.float32, jnp.bfloat16
MESH = pl.DeviceIdType.MESH

RANK = 256
TILES = 116
HALF = TILES // 2
HC = HALF * 128
FAR_FIRST = (4, 3, 5, 2, 6, 1, 7)

PIECES = (
    ("A", 0, 4, 1),
    ("B", 4, 8, 1),
    ("B", 12, 8, 1),
    ("A", 20, 4, 1),
    ("A", 24, 6, 1),
    ("B", 30, 8, -1),
    ("A", 38, 4, -1),
    ("B", 42, 8, -1),
    ("A", 50, 8, -1),
)
ORDER = (
    "0c", "1c", "2c", "3c", "0mid", "4c", "1mid", "5c",
    "3mid", "6c", "0end", "2mid", "7c", "4mid", "1end", "3end",
    "6mid", "5mid", "8c", "0zsum", "4end", "7mid", "2end", "6end",
    "1xsum", "3zsum", "5end", "8mid", "0ysum", "2xsum", "7end", "3ysum",
    "4zsum", "5xsum", "6zsum", "1zsum", "8end", "0agz", "2zsum", "7xsum",
    "4ysum", "3agz", "5zsum", "1agz", "0fwd", "6ysum", "8zsum", "3fwd",
    "2agz", "7zsum", "1agx", "0fin", "4agz", "8ysum", "5agz", "3fin",
    "6agz", "2agx", "7agz", "1fwd", "4fwd", "5agx", "6fwd", "2fwd",
    "8agz", "7agx", "1fin", "4fin", "6fin", "5fwd", "8fwd", "7fwd",
    "2fin", "5fin", "8fin", "7fin",
)


def keys():
    names = ["sc", "pj", "wb", "m1", "m2", "o", "out"]
    for i, (kind, _, _, _) in enumerate(PIECES):
        names += [f"{i}{n}" for n in ("raw", "r1", "r23", "z", "gz", "g1", "g23")]
        names += [f"{i}y"] if kind == "A" else [f"{i}x", f"{i}gx"]
    return {name: k for k, name in enumerate(names)}


KEYS = keys()


def key_of(name):
    if not name[0].isdigit():
        return KEYS[name]
    i, what = name[0], name[1:]
    if what == "out":
        return KEYS["out"]
    if what[0] == "o":
        return KEYS["o"]
    pairs = dict(raw="raw", r1="r1", r2="r23", r3="r23", g1="g1", g2="g23", g3="g23")
    return KEYS[i + pairs.get(what, what[:-1])]


def send_group(name):
    if not name[0].isdigit():
        return {"sc": "sc", "wb": "wb"}.get(name, "pm")
    i, what = name[0], name[1:]
    if what[0] == "o":
        return "out" if what == "out" else "o"
    return i + ("big" if what in ("raw", "r1", "r2", "r3", "g1", "g2", "g3") else "small")


GROUPS = ["sc", "wb", "pm", "out", "o"]
GROUPS += [f"{i}{n}" for i in range(len(PIECES)) for n in ("big", "small")]
GROUPS = {name: k for k, name in enumerate(GROUPS)}


def extents(tiles):
    for bb in (4, 3, 2, 1):
        for cc in (4, 3, 2, 1):
            if tiles % (bb * cc) == 0 and tiles // (bb * cc) <= HALF:
                return tiles // (bb * cc), bb, cc
    raise ValueError(tiles)


def scratch():
    v = pltpu.VMEM
    shapes = dict(
        V=v((2, RANK, HC), bf16),
        SC0=v((RANK, TILES), bf16),
        SC1=v((RANK, TILES), bf16),
        PJ=v((2, 32, RANK), bf16),
        PL=v((RANK, RANK), bf16),
        PT=v((RANK, RANK), bf16),
        SR=v((2, TILES, RANK), bf16),
        RE=v((64, RANK), bf16),
        WB=v((2, 32, HC), bf16),
        NW=v((2, 32, HC), bf16),
        M1=v((2, 8, HC), f32),
        M2=v((2, 8, HC), f32),
        S=v((HALF, 4, 4, 16, 128), bf16),
        G=v((HALF, 4, 4, 16, 128), bf16),
        ssem=pltpu.SemaphoreType.DMA((len(GROUPS),)),
        rsem=pltpu.SemaphoreType.DMA((len(KEYS),)),
        near=pltpu.SemaphoreType.REGULAR((3,)),
    )
    for i, (kind, _, w, _) in enumerate(PIECES):
        if kind == "A":
            part, n = (w, 4, 16, 128), w // 2
            shapes[f"X{i}"] = v((w, 4, 16, 128), bf16)
            shapes[f"RY{i}"] = v((4, n, 16, 128), bf16)
        else:
            q = w // 4
            part, n = (q, 4, 4, 16, 128), q // 2
            shapes[f"Y{i}"] = v(part, bf16)
            shapes[f"RX{i}"] = v((4, q, 4, 16, 128), bf16)
            shapes[f"X{i}"] = v((q, 4, 16, 128), bf16)
        shapes[f"R1{i}"] = shapes[f"T{i}"] = v(part, bf16)
        shapes[f"R23{i}"] = v((2,) + part, bf16)
        shapes[f"RZ{i}"] = v((8, n, 16, 128), bf16)
        shapes[f"OW{i}"] = v((2, 8, n * 128), f32)
    return shapes


def kernel(names, owner, vals, scales, proj, weights, m1, m2, out_w, out_o, *refs):
    r = dict(zip(names, refs))
    S, G = r["S"], r["G"]
    o = lax.axis_index("outer")
    s = lax.axis_index("shard")
    c = lax.rem(s, 2)
    x = lax.rem(lax.div(s, 2), 4)
    zl = lax.div(s, 8)
    y = lax.rem(o, 4)
    zh = lax.div(o, 4)
    z = zh * 4 + zl

    def xi(d):
        return lax.rem(x + d + 4, 4)

    def yi(d):
        return lax.rem(y + d + 4, 4)

    def zi(d):
        return lax.rem(z + d + 8, 8)

    def dev(dx=0, dy=0, dz=0, dc=0):
        zz = zi(dz)
        cc = lax.rem(c + dc, 2)
        return (lax.div(zz, 4) * 4 + yi(dy), lax.rem(zz, 4) * 8 + xi(dx) * 2 + cc)

    def col(core, tile):
        return pl.multiple_of(core * HC + tile * 128, 128)

    sent = {}

    def make(name, src, dst, to):
        return pltpu.make_async_remote_copy(
            src_ref=src,
            dst_ref=dst,
            send_sem=r["ssem"].at[GROUPS[send_group(name)]],
            recv_sem=r["rsem"].at[key_of(name)],
            device_id=to,
            device_id_type=MESH,
        )

    def send(name, src, dst, **to):
        copy = make(name, src, dst, dev(**to))
        copy.start()
        group = send_group(name)
        size = math.prod(src.shape) * src.dtype.itemsize
        sent[group] = sent.get(group, 0) + size

    def got(name, dst):
        pltpu.make_async_copy(dst, dst, r["rsem"].at[key_of(name)]).wait()

    def local(name, src, dst):
        pltpu.make_async_copy(src, dst, r["rsem"].at[key_of(name)]).start()

    barrier = pltpu.get_barrier_semaphore()
    six = [dict(dx=1), dict(dx=-1), dict(dy=1), dict(dy=-1), dict(dz=1), dict(dz=-1)]
    for to in six + [dict(dc=1)]:
        pl.semaphore_signal(barrier, inc=1, device_id=dev(**to), device_id_type=MESH)

    local("sc", scales, r["SR"].at[0])
    for i, (_, off, w, _) in enumerate(PIECES):
        local(
            f"{i}raw",
            vals.at[:, pl.ds(col(c, off), w * 128)],
            r["V"].at[0, :, pl.ds(off * 128, w * 128)],
        )
    local("pj", proj, r["PJ"].at[c])
    local("wb", weights.at[:, pl.ds(col(c, 0), HC)], r["WB"].at[c])
    local("m1", m1.at[:, pl.ds(col(c, 0), HC)], r["M1"].at[c])
    local("m2", m2.at[:, pl.ds(col(c, 0), HC)], r["M2"].at[c])

    pl.semaphore_wait(barrier, 7)
    pc = 1 - c
    send("sc", scales, r["SR"].at[1], dc=1)
    for i, (_, off, w, _) in enumerate(PIECES):
        send(
            f"{i}raw",
            vals.at[:, pl.ds(col(pc, off), w * 128)],
            r["V"].at[1, :, pl.ds(off * 128, w * 128)],
            dc=1,
        )
    send("pj", proj, r["PJ"].at[c], dc=1)
    send("m1", m1.at[:, pl.ds(col(pc, 0), HC)], r["M1"].at[c], dc=1)
    send("m2", m2.at[:, pl.ds(col(pc, 0), HC)], r["M2"].at[c], dc=1)
    send("wb", weights.at[:, pl.ds(col(pc, 0), HC)], r["WB"].at[c], dc=1)

    def near_signal(k):
        for to in six if k == 0 else six[4:]:
            pl.semaphore_signal(
                r["near"].at[k], inc=1, device_id=dev(**to), device_id_type=MESH
            )

    def near_wait(k):
        pl.semaphore_wait(r["near"].at[k], 6 if k == 0 else 2)

    near_signal(0)

    rows = lax.broadcasted_iota(jnp.int32, (1, RANK), 1)
    keys = jnp.broadcast_to((owner[...] * RANK + rows).astype(f32), (RANK, RANK))
    keys_t = keys.T
    place = jnp.sum(jnp.where(keys_t < keys, 1.0, 0.0), axis=0, keepdims=True)
    lines = lax.broadcasted_iota(jnp.int32, (RANK, RANK), 0).astype(f32)
    r["PL"][...] = jnp.where(place == lines, 1.0, 0.0).astype(bf16)
    place_t = jnp.sum(jnp.where(keys < keys_t, 1.0, 0.0), axis=1, keepdims=True)
    lanes = lax.broadcasted_iota(jnp.int32, (RANK, RANK), 1).astype(f32)
    r["PT"][...] = jnp.where(place_t == lanes, 1.0, 0.0).astype(bf16)

    def total(terms):
        out = terms[0].astype(f32)
        for term in terms[1:]:
            out = out + term.astype(f32)
        return out

    def compute(i):
        _, off, w, _ = PIECES[i]
        got(f"{i}raw", r["V"].at[:, :, pl.ds(off * 128, w * 128)])

        def body(j, carry):
            cols = pl.ds(pl.multiple_of((off + 2 * j) * 128, 256), 256)
            block = lax.broadcasted_iota(jnp.int32, (TILES, 256), 0)
            lane = lax.broadcasted_iota(jnp.int32, (TILES, 256), 1)
            want = c * HALF + off + 2 * j + jnp.where(lane >= 128, 1, 0)
            spread = jnp.where(block == want, 1.0, 0.0).astype(bf16)
            e0 = jnp.dot(r["SC0"][...], spread, preferred_element_type=f32)
            e1 = jnp.dot(r["SC1"][...], spread, preferred_element_type=f32)
            both = r["V"][0, :, cols].astype(f32) * e0 + r["V"][1, :, cols].astype(f32) * e1
            put = jnp.dot(r["PL"][...], both.astype(bf16), preferred_element_type=f32)
            put = put.astype(bf16)
            S[off + 2 * j] = put[:, :128].reshape(4, 4, 16, 128)
            S[off + 2 * j + 1] = put[:, 128:].reshape(4, 4, 16, 128)
            return carry

        lax.fori_loop(0, w // 2, body, 0)

    def ring(i):
        kind, off, w, sg = PIECES[i]
        if kind == "A":
            return sg, xi, (lambda d: dict(dx=d)), (lambda b, p: b.at[pl.ds(off, w), :, p])
        q = w // 4
        return sg, yi, (lambda d: dict(dy=d)), (lambda b, p: b.at[pl.ds(off + p * q, q)])

    def piece_loop(n, body):
        def step(t, carry):
            body(t)
            return carry

        lax.fori_loop(0, n, step, 0)

    def start(i):
        sg, at, to, part = ring(i)
        send(f"{i}r1", part(S, at(2 * sg)), r[f"R1{i}"], **to(sg))
        send(f"{i}r3", part(S, at(-sg)), r[f"R23{i}"].at[1], **to(-sg))

    def own_part(i):
        kind, off, w, _ = PIECES[i]
        if kind == "A":
            return w, lambda p, t: S[off + t, :, p]
        q = w // 4
        return q, lambda p, t: S[off + p * q + t]

    def mid(i):
        sg, at, to, part = ring(i)
        got(f"{i}r1", r[f"R1{i}"])
        n, own = own_part(i)
        p = at(sg)

        def body(t):
            r[f"T{i}"][t] = total([own(p, t), r[f"R1{i}"][t]]).astype(bf16)

        piece_loop(n, body)
        send(f"{i}r2", r[f"T{i}"], r[f"R23{i}"].at[0], **to(sg))

    def end(i):
        kind = PIECES[i][0]
        got(f"{i}r3", r[f"R23{i}"])
        n, own = own_part(i)
        p = x if kind == "A" else y
        dst = r[f"X{i}"] if kind == "A" else r[f"Y{i}"]

        def body(t):
            dst[t] = total([own(p, t), r[f"R23{i}"][0, t], r[f"R23{i}"][1, t]]).astype(bf16)

        piece_loop(n, body)
        if kind == "A":
            z_send(i)
        else:
            for k in range(1, 4):
                send(f"{i}x{k}", dst.at[:, :, xi(k)], r[f"RX{i}"].at[x], dx=k)

    def xsum(i):
        got(f"{i}x1", r[f"RX{i}"].at[pl.ds(0, 3)])

        def body(t):
            terms = [r[f"Y{i}"][t, :, x]] + [r[f"RX{i}"][xi(-k), t] for k in range(1, 4)]
            r[f"X{i}"][t] = total(terms).astype(bf16)

        piece_loop(PIECES[i][2] // 4, body)
        z_send(i)

    def z_tiles(i):
        kind, _, w, _ = PIECES[i]
        return w // 2 if kind == "A" else w // 8

    def z_send(i):
        n = z_tiles(i)
        for k in FAR_FIRST:
            zz = zi(k)
            src = r[f"X{i}"].at[pl.ds(lax.div(zz, 4) * n, n), lax.rem(zz, 4)]
            send(f"{i}z{k}", src, r[f"RZ{i}"].at[z], dz=k)

    def z_terms(i, t):
        n = z_tiles(i)
        terms = [r[f"X{i}"][zh * n + t, zl]]
        return terms + [r[f"RZ{i}"][zi(-k), t] for k in range(1, 8)]

    def z_got(i):
        got(f"{i}z1", r[f"RZ{i}"].at[pl.ds(0, 7)])

    def first_tile(i, yy, hh):
        kind, off, w, _ = PIECES[i]
        if kind == "A":
            return off + hh * (w // 2)
        return off + yy * (w // 4) + hh * (w // 8)

    def update(i, owned_of):
        n = z_tiles(i)
        tile0 = first_tile(i, y, zh)

        def body(t):
            owned = owned_of(t)
            cols = pl.ds(pl.multiple_of((tile0 + t) * 128, 128), 128)
            dirs = []
            for h in range(2):
                part = owned[8 * h : 8 * h + 8]
                r[f"OW{i}"][h, :, pl.ds(pl.multiple_of(t * 128, 128), 128)] = part
                nf = first_decay * r["M1"][h, :, cols] + (1.0 - first_decay) * part
                ns = second_decay * r["M2"][h, :, cols] + (1.0 - second_decay) * part * part
                corrected = nf / (1.0 - first_decay**step_count)
                spread = jnp.sqrt(ns / (1.0 - second_decay**step_count)) + 1e-08
                dirs.append(corrected / spread)
            G[tile0 + t, zl, x] = jnp.concatenate(dirs, axis=0).astype(bf16)

        piece_loop(n, body)
        mine = G.at[pl.ds(tile0, n), zl, x]
        for k in FAR_FIRST:
            send(f"{i}gz{k}", mine, mine, dz=k)

    def owned_send(i):
        n = z_tiles(i)
        tile0 = first_tile(i, y, zh)
        cols = pl.ds(col(c, tile0), n * 128)
        local(f"{i}o000", r[f"OW{i}"].at[c], out_o.at[:, cols])
        for dy in range(4 if PIECES[i][0] == "B" else 1):
            for dz in range(2):
                for dc in range(2):
                    if dy + dz + dc:
                        src = r[f"OW{i}"].at[pc if dc else c]
                        send(
                            f"{i}o{dy}{dz}{dc}", src, out_o.at[:, cols], dy=dy, dz=4 * dz, dc=dc
                        )

    def zsum_a(i):
        z_got(i)

        def body(t):
            r[f"RY{i}"][y, t] = total(z_terms(i, t)).astype(bf16)

        piece_loop(z_tiles(i), body)
        for k in range(1, 4):
            send(f"{i}y{k}", r[f"RY{i}"].at[y], r[f"RY{i}"].at[y], dy=k)

    def ysum(i):
        got(f"{i}y1", r[f"RY{i}"].at[pl.ds(0, 3)])
        update(i, lambda t: total([r[f"RY{i}"][k, t] for k in range(4)]))

    def zsum_b(i):
        z_got(i)
        update(i, lambda t: total(z_terms(i, t)))

    def gather_z_got(i):
        a, bb, cc = extents(7 * z_tiles(i))
        got(f"{i}gz1", S.at[pl.ds(0, a), pl.ds(0, bb), pl.ds(0, cc)])

    def last_ring(i):
        sg, at, to, part = ring(i)
        mine = part(G, at(0))
        send(f"{i}g1", mine, mine, **to(sg))
        send(f"{i}g3", mine, mine, **to(-sg))

    def agz(i):
        gather_z_got(i)
        kind, off, w, _ = PIECES[i]
        if kind == "A":
            last_ring(i)
        else:
            q = w // 4
            mine = G.at[pl.ds(off + y * q, q), :, x]
            for k in range(1, 4):
                send(f"{i}gx{k}", mine, mine, dx=k)

    def agx(i):
        _, off, w, _ = PIECES[i]
        q = w // 4
        got(f"{i}gx1", G.at[pl.ds(off, q), :, pl.ds(0, 3)])
        last_ring(i)

    def fwd(i):
        sg, at, to, part = ring(i)
        behind = part(G, at(-sg))
        got(f"{i}g1", behind)
        send(f"{i}g2", behind, behind, **to(sg))
        owned_send(i)

    def fin(i):
        _, off, w, _ = PIECES[i]
        sg, at, to, part = ring(i)
        if PIECES[i][0] == "A":
            got(f"{i}g3", G.at[pl.ds(off, w), :, pl.ds(0, 2)])
        else:
            got(f"{i}g3", G.at[pl.ds(off, w // 2)])

        def body(j, carry):
            cols = pl.ds(pl.multiple_of((off + 2 * j) * 128, 256), 256)
            u = jnp.concatenate(
                [G[off + 2 * j].reshape(256, 128), G[off + 2 * j + 1].reshape(256, 128)], axis=1
            )
            change = jnp.dot(r["RE"][...], u, preferred_element_type=f32)
            old = r["WB"][:, :, cols].reshape(64, 256).astype(f32)
            new = (old - update_scale * change).astype(bf16)
            r["NW"][:, :, cols] = new.reshape(2, 32, 256)
            return carry

        lax.fori_loop(0, w // 2, body, 0)
        here = pl.ds(off * 128, w * 128)
        there = pl.ds(col(c, off), w * 128)
        send(f"{i}out", r["NW"].at[pc, :, here], out_w.at[:, there], dc=1)
        local(f"{i}out", r["NW"].at[c, :, here], out_w.at[:, there])

    actions = dict(
        mid=mid, end=end, xsum=xsum, ysum=ysum, agz=agz, agx=agx, fwd=fwd, fin=fin
    )
    got("sc", r["SR"])
    for k in range(2):
        r[f"SC{k}"][...] = r["SR"][k].astype(f32).T.astype(bf16)
    rounds = 0
    updating = {"A": "ysum", "B": "zsum"}
    have_moments = have_weights = False
    for item in ORDER:
        i, what = int(item[0]), item[1:]
        if what == updating[PIECES[i][0]] and not have_moments:
            have_moments = True
            got("m1", r["M1"])
            got("m2", r["M2"])
        if what == "fin" and not have_weights:
            have_weights = True
            got("pj", r["PJ"])
            got("wb", r["WB"])
            reordered = jnp.dot(
                r["PJ"][...].reshape(64, RANK), r["PT"][...], preferred_element_type=f32
            )
            r["RE"][...] = reordered.astype(bf16)
        if what == "c":
            compute(i)
            start(i)
        elif what == "zsum":
            (zsum_a if PIECES[i][0] == "A" else zsum_b)(i)
        else:
            actions[what](i)

        if rounds < 3:
            near_wait(rounds)
            if rounds < 2:
                near_signal(rounds + 1)
        rounds += 1

    got("o", out_o)
    got("out", out_w)
    for group, size in sent.items():
        if group == "sc":
            whole = r["SR"].at[0]
        else:
            a, bb, cc = extents(size // 4096)
            whole = S.at[pl.ds(0, a), pl.ds(0, bb), pl.ds(0, cc)]
        pltpu.make_async_copy(whole, whole, r["ssem"].at[GROUPS[group]]).wait()


def moments_kernel(weights, owned, first, second, new_weights, new_first, new_second):
    new_weights[...] = weights[...]
    grad = owned[...]
    new_first[...] = first_decay * first[...] + (1.0 - first_decay) * grad
    new_second[...] = second_decay * second[...] + (1.0 - second_decay) * grad * grad


def per_device(
    grad_values, grad_scales, block_owner, projector, weights, first_moment, second_moment
):
    shapes = scratch()
    any_spec = pl.BlockSpec(memory_space=pl.ANY)
    new_weights, owned = pl.pallas_call(
        functools.partial(kernel, tuple(shapes)),
        out_shape=(
            jax.ShapeDtypeStruct(weights.shape, bf16),
            jax.ShapeDtypeStruct(first_moment.shape, f32),
        ),
        in_specs=[pl.BlockSpec(memory_space=pltpu.VMEM)] + [any_spec] * 6,
        out_specs=(any_spec, any_spec),
        scratch_shapes=list(shapes.values()),
        compiler_params=pltpu.CompilerParams(
            collective_id=0, has_side_effects=True, vmem_limit_bytes=60 * 1024 * 1024
        ),
    )(
        block_owner.reshape(1, RANK),
        grad_values[0, 0],
        grad_scales[0, 0].T,
        projector,
        weights,
        first_moment,
        second_moment,
    )
    steps = 2
    width = first_moment.shape[1] // steps

    def column_block(array):
        return pl.BlockSpec((array.shape[0], width), lambda j: (0, j))

    ins = (new_weights, owned, first_moment, second_moment)
    outs = (new_weights, first_moment, second_moment)
    new_weights, new_first, new_second = pl.pallas_call(
        moments_kernel,
        grid=(steps,),
        out_shape=tuple(jax.ShapeDtypeStruct(a.shape, a.dtype) for a in outs),
        in_specs=[column_block(a) for a in ins],
        out_specs=tuple(column_block(a) for a in outs),
        cost_estimate=pl.CostEstimate(flops=800000, bytes_accessed=4300000, transcendentals=0),
    )(*ins)
    return (new_weights, new_first, new_second)


def solution(mesh):
    placed = (
        P("outer", "shard", None, None),
        P("outer", "shard", None, None),
        P(),
        P(("outer", "shard"), None),
        P(("outer", "shard"), None),
        P("shard", None),
        P("shard", None),
    )
    return jax.shard_map(
        per_device,
        mesh=mesh,
        in_specs=placed,
        out_specs=(P(("outer", "shard"), None), P("shard", None), P("shard", None)),
        check_vma=False,
    )
```
